256 devices in a mesh: segment: 8 (over z), expert: 32 (over y, x, core).
Axes of the slice: x: 4, y: 4, z: 8, core: 2. Of those that a mesh axis runs over, the one named last changes fastest.
Arguments:
- inputs: bfloat16 [8, 2, 4096, 2048], P('segment', None, 'expert'), may hold values from -6 to 6
- entering: bfloat16 [8, 4096, 2048], P('segment', 'expert'), may hold values from -6 to 6
- weight_in: bfloat16 [8, 32, 704, 2048], P('segment', 'expert'), may hold values from -0.125 to 0.125
- weight_out: bfloat16 [8, 32, 704, 2048], P('segment', 'expert'), may hold values from -0.21875 to 0.21875
- gate_probs: bfloat16 [8, 2, 4096, 2], P('segment', None, 'expert'), may hold values from 0.049804688 to 1
- expert_ids: int32 [8, 2, 4096, 2], P('segment', None, 'expert'), may hold values from 0 to 31, as said below
Outputs:
- grad_in: bfloat16 [8, 32, 704, 2048], P('segment', 'expert')
- grad_out: bfloat16 [8, 32, 704, 2048], P('segment', 'expert')
- prob_grads: bfloat16 [8, 2, 4096, 2], P('segment', None, 'expert')
The draws below stay inside these ranges and needn't reach their ends.
Inputs may be any that keep to these rules, and one draw needn't show every extreme that they name: `expert_ids`: each token names 2 different experts. In each aligned block of 128 tokens of one section and tick no expert is named by more than 12 tokens, and in every section and tick one expert, the same for all blocks of that section and tick, is named by exactly 12 tokens of every block.
All inputs are finite; a program needn't handle non-finite values.
Results may differ from the reference program's by a relative error of at most 0.0085.
Values may be sent and summed in bfloat16 or wider, within the bound.
A program may use at most 128 MiB of HBM per device.

```python
import math
import jax
import jax.numpy as jnp
from jax import lax

D = 2048
FF = 704
TOPK = 2
TICKS = 2
TOK_DEV = 128
SEGMENTS = 8
EXPERTS = 32
TOKENS = 4096
CAP = 12


def draw_expert_ids(key, part):
    blocks = TOKENS // TOK_DEV
    candidates = EXPERTS * CAP
    hot_expert = jax.random.randint(jax.random.fold_in(key, 7), (SEGMENTS, TICKS), 0, EXPERTS)
    hot_expert = jnp.broadcast_to(hot_expert[:, :, None], (SEGMENTS, TICKS, blocks)).reshape(-1)
    block_count = SEGMENTS * TICKS * blocks
    block_keys = jax.random.split(jax.random.fold_in(key, 11), block_count)

    def one_block(block_key, hot_one):
        key_bias, key_score, key_rows = jax.random.split(block_key, 3)
        positions = jnp.arange(candidates, dtype=jnp.int32)
        owner = positions // CAP
        owner_bias = jax.random.randint(key_bias, (EXPERTS,), 0, 4)
        score = jax.random.randint(key_score, (candidates,), 0, 1 << 16)
        score = (score + owner_bias[owner] * (1 << 16)) * candidates + positions
        score = jnp.where(owner == hot_one, -1 - positions, score)
        ranking = jnp.argsort(score)
        chosen = jnp.sort(owner[ranking[:TOK_DEV * TOPK]])
        row_pairs = chosen.reshape(TOPK, TOK_DEV).T
        return row_pairs[jax.random.permutation(key_rows, TOK_DEV)]
    drawn = jax.vmap(one_block)(block_keys, hot_expert)
    return drawn.reshape(SEGMENTS, TICKS, TOKENS, TOPK).astype(jnp.int32)


def level_of(own_key, extent, cuts, low, high):
    def one(axis_at, parts):
        draws = jax.random.uniform(jax.random.fold_in(jax.random.fold_in(own_key, 6), axis_at), (parts,), jnp.float32, low / len(cuts), high / len(cuts))
        return jnp.repeat(jnp.exp(draws), extent[axis_at] // parts).reshape((-1,) + (1,) * (len(extent) - axis_at - 1))

    factor_of = one(*cuts[0])
    for cut in cuts[1:]:
        factor_of = factor_of * one(*cut)
    return factor_of


def scatter_about(key, extent, scale, limit, cuts=(), held_as=jnp.bfloat16):
    gain = level_of(key, extent, cuts, -0.22, 0.18) if cuts else 1.0
    result = jax.random.normal(key, extent, jnp.float32) * scale * gain
    return jnp.minimum(jnp.maximum(result, -limit), limit).astype(held_as)


def setup_inputs(seed: int = 0) -> dict:
    splits = jax.random.split(jax.random.key(seed), 7)
    return {
        "inputs": scatter_about(splits[0], (SEGMENTS, TICKS, TOKENS, D), 1.0, 6.0, ((0, 8), (2, 32))),
        "entering": scatter_about(splits[1], (SEGMENTS, TOKENS, D), 1.0, 6.0, ((0, 8), (1, 32))),
        "weight_in": scatter_about(splits[2], (SEGMENTS, EXPERTS, FF, D), D ** -0.5, 0.125, ((0, 8), (1, 32))),
        "weight_out": scatter_about(splits[3], (SEGMENTS, EXPERTS, FF, D), FF ** -0.5, 0.21875, ((0, 8), (1, 32))),
        "gate_probs": jnp.clip(jnp.exp(math.log(1.0) - 2.9996462 * jax.random.uniform(splits[4], (SEGMENTS, TICKS, TOKENS, TOPK), jnp.float32) ** level_of(splits[4], (SEGMENTS, TICKS, TOKENS, TOPK), ((0, 8), (2, 32)), -0.2, 0.2)), 0.049804688, 1.0).astype(jnp.bfloat16),
        "expert_ids": draw_expert_ids(jax.random.fold_in(splits[6], 71), 0),
    }


half_root = 0.7071067811865476
density_scale = 0.3989422804014327


def gelu_parts(preact):
    normal_cdf = 0.5 * (1.0 + jax.scipy.special.erf(preact * half_root))
    normal_pdf = density_scale * jnp.exp(-0.5 * preact * preact)
    return preact * normal_cdf, normal_cdf + preact * normal_pdf


def segment_tick(rows_in, incoming, w_in, w_out, probs, chosen):
    sources = TOKENS // TOK_DEV
    per_source = chosen.reshape(sources, TOK_DEV * TOPK).astype(jnp.int32)
    matches = (per_source[:, :, None] == jnp.arange(EXPERTS, dtype=jnp.int32)[None, None, :]).astype(jnp.int32)
    before = jnp.cumsum(matches, axis=1) - matches
    rank_in = jnp.sum(before * matches, axis=2).astype(jnp.int32)
    source_grid = jnp.broadcast_to(jnp.arange(sources, dtype=jnp.int32)[:, None], rank_in.shape)
    token_at = (source_grid * TOK_DEV + jnp.arange(TOK_DEV * TOPK, dtype=jnp.int32)[None, :] // TOPK).reshape(-1)
    source_at = source_grid.reshape(-1)
    expert_at = per_source.reshape(-1)
    slot_at = rank_in.reshape(-1)
    features = rows_in.shape[1]
    slots_x = jnp.zeros((EXPERTS, sources, CAP, features), rows_in.dtype).at[expert_at, source_at, slot_at].set(rows_in[token_at])
    slots_g = jnp.zeros((EXPERTS, sources, CAP, features), incoming.dtype).at[expert_at, source_at, slot_at].set(incoming[token_at])
    slots_p = jnp.zeros((EXPERTS, sources, CAP), probs.dtype).at[expert_at, source_at, slot_at].set(probs.reshape(-1))
    rows_x = slots_x.reshape(EXPERTS, sources * CAP, features).astype(jnp.float32)
    rows_g = slots_g.reshape(EXPERTS, sources * CAP, features).astype(jnp.float32)
    rows_p = slots_p.reshape(EXPERTS, sources * CAP, 1).astype(jnp.float32)
    weights_in = w_in.astype(jnp.float32)
    weights_out = w_out.astype(jnp.float32)
    preact = jnp.einsum("erd,efd->erf", rows_x, weights_in)
    activated, gate_slope = gelu_parts(preact)
    hidden = lax.optimization_barrier(activated.astype(jnp.bfloat16)).astype(jnp.float32)
    pulled = jnp.einsum("erd,efd->erf", rows_g, weights_out)
    scores = jnp.sum(hidden * pulled, axis=2).astype(jnp.bfloat16)
    grad_pre = lax.optimization_barrier((rows_p * pulled * gate_slope).astype(jnp.bfloat16)).astype(jnp.float32)
    grad_y = lax.optimization_barrier((rows_p * rows_g).astype(jnp.bfloat16)).astype(jnp.float32)
    part_out = jnp.einsum("erf,erd->efd", hidden, grad_y)
    part_in = jnp.einsum("erf,erd->efd", grad_pre, rows_x)
    returned = jnp.einsum("erf,efd->erd", grad_pre, weights_in).astype(jnp.bfloat16)
    returned = lax.optimization_barrier(returned).reshape(EXPERTS, sources, CAP, features)
    picked = returned[expert_at, source_at, slot_at].astype(jnp.float32).reshape(TOKENS, TOPK, features)
    leaving = (incoming.astype(jnp.float32) + jnp.sum(picked, axis=1)).astype(jnp.bfloat16)
    prob_part = scores.reshape(EXPERTS, sources, CAP)[expert_at, source_at, slot_at].reshape(TOKENS, TOPK)
    return leaving, part_in, part_out, prob_part


def reference(inputs, entering, weight_in, weight_out, gate_probs, expert_ids):
    def per_segment(from_next, pieces):
        rows_all, entering_one, w_in, w_out, probs_all, chosen_all = pieces
        total_in = jnp.zeros((EXPERTS, FF, D), jnp.float32)
        total_out = jnp.zeros((EXPERTS, FF, D), jnp.float32)
        produced = []
        prob_list = []
        incoming = entering_one
        for moment in range(TICKS):
            if moment > 0:
                incoming = from_next[moment - 1]
            leaving, part_in, part_out, prob_part = segment_tick(rows_all[moment], incoming, w_in, w_out, probs_all[moment], chosen_all[moment])
            total_in = total_in + part_in
            total_out = total_out + part_out
            produced.append(leaving)
            prob_list.append(prob_part)
        carry_out = jnp.stack(produced[:TICKS - 1])
        return carry_out, (total_in.astype(jnp.bfloat16), total_out.astype(jnp.bfloat16), jnp.stack(prob_list))

    start_carry = jnp.zeros((TICKS - 1, TOKENS, D), entering.dtype)
    unused_carry, outputs = lax.scan(per_segment, start_carry, (inputs, entering, weight_in, weight_out, gate_probs, expert_ids), reverse=True)
    return outputs[0], outputs[1], outputs[2]
```

```python
import jax
import jax.numpy as jnp
from jax import lax
from jax.experimental import pallas as pl
from jax.experimental.pallas import tpu as pltpu
from jax.sharding import PartitionSpec as P

MESH = pl.DeviceIdType.MESH
F32 = jnp.float32
BF16 = jnp.bfloat16
NT = (((1,), (1,)), ((), ()))
FF = 704
D = 2048
TOK = 128
PEERS = 32
ROWS = 256
WIDE = 3072
HALF = 192
HR = 0.7071067811865476
DS = 0.3989422804014327


def iota(shape, dim):
    return lax.broadcasted_iota(jnp.int32, shape, dim)


def dot(a, b):
    return jnp.dot(a, b, preferred_element_type=F32)


def dot_nt(a, b):
    return lax.dot_general(a, b, NT, preferred_element_type=F32)


def onehot(cond):
    return jnp.where(cond, 1.0, 0.0)


def kernel(
    inputs_hbm, entering_hbm, win_hbm, wout_hbm, probs_ref, ids_ref,
    gin_hbm, gout_hbm, pg_ref,
    xin, g0, win, wout,
    sx0, sg, sx1, rs,
    xr0, gr0, xr1, rr, gr1,
    xc, gc, ht, gp, slope, gpr, rb,
    acco, acci, outo, outi,
    lv_send, lv_recv, s_send, s_recv,
    da, dap, ca, cols,
    send_sem, recv_sem, z_send, z_recv, local_sem, out_sem,
):
    me = lax.axis_index("expert")
    seg = lax.axis_index("segment")
    core = lax.rem(me, 2)
    px = lax.rem(lax.div(me, 2), 4)
    py = lax.div(me, 8)

    def steps(k):
        dc = lax.rem(k, 2)
        dx = lax.rem(lax.div(k, 2), 4)
        dy = lax.rem(lax.div(k, 8) + dx, 4)
        return dy, dx, dc

    def ahead(k):
        dy, dx, dc = steps(k)
        return lax.rem(py + dy, 4) * 8 + lax.rem(px + dx, 4) * 2 + lax.rem(core + dc, 2)

    def behind(k):
        dy, dx, dc = steps(k)
        return lax.rem(py + 4 - dy, 4) * 8 + lax.rem(px + 4 - dx, 4) * 2 + lax.rem(core + dc, 2)

    def copy(stage, src, dst, k, peer):
        rows = pl.ds(pl.multiple_of(k * 8, 8), 8)
        return pltpu.make_async_remote_copy(
            src_ref=src.at[rows], dst_ref=dst.at[rows],
            send_sem=send_sem.at[stage, k], recv_sem=recv_sem.at[stage, k],
            device_id=(seg, peer), device_id_type=MESH,
        )

    def send(stage, src, dst, route, low, high):
        def one(k, carry):
            copy(stage, src, dst, k, route(k)).start()
            return carry
        lax.fori_loop(max(low, 1), high, one, 0)

    def arrive(stage, src, dst, low, high):
        def one(k, carry):
            copy(stage, src, dst, k, ahead(k)).wait_recv()
            return carry
        lax.fori_loop(max(low, 1), high, one, 0)

    def sent(stage, src, dst):
        def one(k, carry):
            copy(stage, src, dst, k, ahead(k)).wait_send()
            return carry
        lax.fori_loop(1, PEERS, one, 0)

    load_g = pltpu.make_async_copy(entering_hbm, g0, local_sem.at[0])
    load_x = pltpu.make_async_copy(inputs_hbm, xin, local_sem.at[1])
    load_wi = pltpu.make_async_copy(win_hbm, win, local_sem.at[2])
    load_wo = pltpu.make_async_copy(wout_hbm, wout, local_sem.at[3])
    load_x.start()
    load_g.start()
    load_wi.start()
    load_wo.start()

    barrier = pltpu.get_barrier_semaphore()

    def greet(k, carry):
        pl.semaphore_signal(barrier, inc=1, device_id=(seg, ahead(k)), device_id_type=MESH)
        return carry

    lax.fori_loop(1, PEERS, greet, 0)
    below = lax.rem(seg + 7, 8)
    above = lax.rem(seg + 1, 8)
    pl.semaphore_signal(barrier, inc=1, device_id=(below, me), device_id_type=MESH)
    pl.semaphore_signal(barrier, inc=1, device_id=(above, me), device_id_type=MESH)

    def places(tick):
        ids = ids_ref[tick]
        k = iota((TOK, 128), 1)
        dx = (k >> 1) & 3
        dy = ((k >> 3) + dx) & 3
        owner = ((py + dy) & 3) * 8 + ((px + dx) & 3) * 2 + ((core + (k & 1)) & 1)
        owner = jnp.where(k < PEERS, owner, -1)
        named = [ids[:, j : j + 1] == owner for j in range(2)]
        either = onehot(named[0] | named[1]).astype(BF16)
        earlier = onehot(iota((TOK, TOK), 1) < iota((TOK, TOK), 0)).astype(BF16)
        count = dot(earlier, either)
        first = (k * 8).astype(F32)
        probs = probs_ref[tick].astype(F32)
        packed = jnp.zeros((TOK, 128), F32)
        for j in range(2):
            rank = jnp.sum(jnp.where(named[j], count, 0.0), axis=1, keepdims=True)
            base = jnp.sum(jnp.where(named[j], first, 0.0), axis=1, keepdims=True)
            low = jnp.where(rank < 8.0, base + rank, -100.0)
            high = jnp.where(rank < 8.0, -100.0, base + rank - 8.0)
            packed = jnp.where(k == j, low, packed)
            packed = jnp.where(k == 2 + j, high, packed)
            packed = jnp.where(k == 4 + j, probs[:, j : j + 1], packed)
        cols[tick] = packed
        eye = onehot(iota((8, 128), 0) == iota((8, 128), 1)).astype(BF16)
        turned = dot_nt(eye, packed.astype(BF16))
        slot = iota((ROWS, TOK), 0).astype(F32)
        for part, (row, shift) in enumerate(((0, 0.0), (2, 0.0), (2, 4.0))):
            hit0 = slot == turned[row : row + 1] + shift
            hit1 = slot == turned[row + 1 : row + 2] + shift
            da[part] = onehot(hit0 | hit1).astype(BF16)
            dap[part] = jnp.where(
                hit0, turned[4:5], jnp.where(hit1, turned[5:6], 0.0)
            ).astype(BF16)

    def pick(tick, j, part):
        row, shift = ((0, 0.0), (2, 0.0), (2, 4.0))[part]
        slot = iota((TOK, ROWS), 1).astype(F32)
        return slot == cols[tick, :, row + j : row + j + 1] + shift

    def dispatch(mats, rows, dst):
        for n in range(4):
            c = slice(n * 512, n * 512 + 512)
            dst[:, c] = dot(mats[0], rows[:, c]).astype(BF16)
        for n in range(2):
            c = slice(n * 512, n * 512 + 512)
            h = slice(1024 + n * 512, 1536 + n * 512)
            dst[:, 2048 + n * 512 : 2560 + n * 512] = (
                dot(mats[1], rows[:, c]) + dot(mats[2], rows[:, h])
            ).astype(BF16)

    def split_matrix():
        o = iota((128, 128), 0)
        i = iota((128, 128), 1)
        return onehot(i == ((o & 63) >> 2) * 8 + (o >> 6) * 4 + (o & 3)).astype(BF16)

    def join_matrix():
        i = iota((128, 128), 0)
        o = iota((128, 128), 1)
        return onehot(i == ((o & 63) >> 2) * 8 + (o >> 6) * 4 + (o & 3)).astype(BF16)

    def gather(src, dst, tick, h):
        r = slice(h * 128, h * 128 + 128)
        dst[tick, h, 0:128, :] = src[r, 0:D]
        for n in range(2):
            b = dot(split_matrix(), src[r, D + n * 512 : D + n * 512 + 512]).astype(BF16)
            dst[tick, h, 128:192, n * 512 : n * 512 + 512] = b[0:64]
            dst[tick, h, 128:192, 1024 + n * 512 : 1536 + n * 512] = b[64:128]

    def forward(tick, h):
        def tile(m, carry):
            r = pl.ds(pl.multiple_of(m * 352, 16), 352)
            pre = dot_nt(win[r, :], xc[tick, h])
            cdf = 0.5 * (1.0 + lax.erf(pre * HR))
            pdf = DS * jnp.exp(-0.5 * pre * pre)
            ht[tick, h, r, :] = (pre * cdf).astype(BF16)
            slope[h, r, :] = cdf + pre * pdf
            return carry
        lax.fori_loop(0, 2, tile, 0)

    def backward(tick, h):
        def tile(m, total):
            r = pl.ds(pl.multiple_of(m * 352, 16), 352)
            q = dot_nt(wout[r, :], gc[tick, h])
            gp[tick, h, r, :] = (q * slope[h, r, :]).astype(BF16)
            return total + jnp.sum(ht[tick, h, r, :].astype(F32) * q, axis=0, keepdims=True)
        s = lax.fori_loop(0, 2, tile, jnp.zeros((1, HALF), F32))
        i = iota((128, HALF), 0)
        r = iota((128, HALF), 1)
        ones = jnp.ones((HALF, 128), BF16)
        sa = dot(jnp.where(r == i, s, 0.0).astype(BF16), ones)
        tail = ((i & 7) < 4) & (r == 128 + (i >> 3) * 4 + (i & 7))
        sb = dot(jnp.where(tail, s, 0.0).astype(BF16), ones)
        lane = iota((128, 128), 1)
        rows = slice(h * 128, h * 128 + 128)
        before = jnp.zeros((128, 128), F32) if tick == 0 else s_send[rows, :].astype(F32)
        s_send[rows, :] = jnp.where(
            lane == tick, sa, jnp.where(lane == 2 + tick, sb, before)
        ).astype(BF16)

    def give_back(h):
        eye = onehot(iota((HALF, HALF), 0) == iota((HALF, HALF), 1)).astype(BF16)
        gpr[...] = dot_nt(eye, gp[0, h]).astype(BF16)
        rows = slice(h * 128, h * 128 + 128)

        def tile(n, carry):
            c = pl.ds(pl.multiple_of(n * 512, 512), 512)
            r = dot(gpr[...], win[:, c]).astype(BF16)
            rs[rows, c] = r[0:128]
            rb[:, c] = r[128:192]
            return carry

        lax.fori_loop(0, 4, tile, 0)
        join = join_matrix()
        for n in range(2):
            c = slice(n * 512, n * 512 + 512)
            d = slice(1024 + n * 512, 1536 + n * 512)
            b = dot(join[:, 0:64], rb[:, c]) + dot(join[:, 64:128], rb[:, d])
            rs[rows, D + n * 512 : D + n * 512 + 512] = b.astype(BF16)

    def own(src, dst):
        dst[0:8, :] = src[0:8, :]

    places(0)
    load_x.wait()
    dispatch([da[0], da[1], da[2]], xin.at[0], sx0)
    pl.semaphore_wait(barrier, PEERS + 1)
    send(0, sx0, xr0, ahead, 0, PEERS)
    load_g.wait()
    dispatch([dap[0], dap[1], dap[2]], g0, sg)
    send(1, sg, gr0, ahead, 0, PEERS)
    own(sx0, xr0)
    own(sg, gr0)
    for part in range(3):
        ca[part] = onehot(pick(0, 0, part) | pick(0, 1, part)).astype(BF16)
    places(1)
    dispatch([da[0], da[1], da[2]], xin.at[1], sx1)
    own(sx1, xr1)
    load_wi.wait()
    load_wo.wait()

    for h in range(2):
        arrive(0, sx0, xr0, h * 16, h * 16 + 16)
        gather(xr0, xc, 0, h)
        forward(0, h)
    for h in range(2):
        arrive(1, sg, gr0, h * 16, h * 16 + 16)
        gather(gr0, gc, 0, h)
        backward(0, h)
        give_back(h)
        send(2, rs, rr, behind, h * 16, h * 16 + 16)
    own(rs, rr)
    send(3, sx1, xr1, ahead, 0, PEERS)

    def first_sums(n, carry):
        c = pl.ds(pl.multiple_of(n * 256, 256), 256)
        acco[:, c] = dot(ht[0, 0], gc[0, 0, :, c]) + dot(ht[0, 1], gc[0, 1, :, c])
        acci[:, c] = dot(gp[0, 0], xc[0, 0, :, c]) + dot(gp[0, 1], xc[0, 1, :, c])
        return carry

    lax.fori_loop(0, 8, first_sums, 0)

    arrive(2, rs, rr, 0, PEERS)
    for n in range(4):
        c = slice(n * 512, n * 512 + 512)
        d = slice(D + (n % 2) * 512, D + (n % 2) * 512 + 512)
        total = g0[:, c].astype(F32) + dot(ca[0], rr[:, c]) + dot(ca[1 + n // 2], rr[:, d])
        lv_send[:, c] = total.astype(BF16)
    relay = pltpu.make_async_remote_copy(
        src_ref=lv_send, dst_ref=lv_recv, send_sem=z_send, recv_sem=z_recv,
        device_id=(below, me), device_id_type=MESH,
    )
    relay.start()
    sent(1, sg, gr0)
    relay.wait_recv()
    for n in range(4):
        c = slice(n * 512, n * 512 + 512)
        v = lv_recv[:, c]
        g0[:, c] = jnp.where(seg == 7, jnp.zeros_like(v), v)
    dispatch([dap[0], dap[1], dap[2]], g0, sg)
    send(4, sg, gr1, ahead, 0, PEERS)
    own(sg, gr1)

    for h in range(2):
        arrive(3, sx1, xr1, h * 16, h * 16 + 16)
        gather(xr1, xc, 1, h)
        forward(1, h)

    arrive(4, sg, gr1, 0, 16)
    gather(gr1, gc, 1, 0)
    backward(1, 0)

    def more_sums(n, carry):
        c = pl.ds(pl.multiple_of(n * 256, 256), 256)
        acco[:, c] += dot(ht[1, 0], gc[1, 0, :, c])
        acci[:, c] += dot(gp[1, 0], xc[1, 0, :, c])
        return carry

    lax.fori_loop(0, 8, more_sums, 0)

    arrive(4, sg, gr1, 16, PEERS)
    gather(gr1, gc, 1, 1)
    backward(1, 1)
    send(5, s_send, s_recv, behind, 0, PEERS)
    own(s_send, s_recv)

    def last_sums(n, carry):
        c = pl.ds(pl.multiple_of(n * 256, 256), 256)
        outo[:, c] = (acco[:, c] + dot(ht[1, 1], gc[1, 1, :, c])).astype(BF16)
        outi[:, c] = (acci[:, c] + dot(gp[1, 1], xc[1, 1, :, c])).astype(BF16)
        pltpu.make_async_copy(outo.at[:, c], gout_hbm.at[:, c], out_sem.at[0, n]).start()
        pltpu.make_async_copy(outi.at[:, c], gin_hbm.at[:, c], out_sem.at[1, n]).start()
        return carry

    lax.fori_loop(0, 8, last_sums, 0)

    arrive(5, s_send, s_recv, 0, PEERS)
    lane = iota((TOK, 128), 1)
    score = s_recv[...]
    for tick in range(2):
        found = []
        for j in range(2):
            va = dot(onehot(pick(tick, j, 0)).astype(BF16), score)
            vb = dot(onehot(pick(tick, j, 1)).astype(BF16), score)
            both = jnp.where(lane == tick, va, 0.0) + jnp.where(lane == 2 + tick, vb, 0.0)
            value = jnp.sum(both, axis=1, keepdims=True)
            found.append(value / cols[tick, :, 4 + j : 5 + j])
        pair = jnp.where(iota((TOK, 2), 1) == 0, found[0], found[1])
        pg_ref[tick] = pair.astype(BF16)

    def out_done(n, carry):
        c = pl.ds(pl.multiple_of(n * 256, 256), 256)
        pltpu.make_async_copy(outo.at[:, c], gout_hbm.at[:, c], out_sem.at[0, n]).wait()
        pltpu.make_async_copy(outi.at[:, c], gin_hbm.at[:, c], out_sem.at[1, n]).wait()
        return carry

    lax.fori_loop(0, 8, out_done, 0)
    relay.wait_send()
    sent(0, sx0, xr0)
    sent(2, rs, rr)
    sent(3, sx1, xr1)
    sent(4, sg, gr1)
    sent(5, s_send, s_recv)


def body(inputs, entering, weight_in, weight_out, gate_probs, expert_ids):
    anyspace = pl.BlockSpec(memory_space=pl.ANY)
    vmem = pl.BlockSpec(memory_space=pltpu.VMEM)
    wide = pltpu.VMEM((ROWS, WIDE), BF16)
    weight = pltpu.VMEM((FF, D), BF16)
    grad = jax.ShapeDtypeStruct((FF, D), BF16)
    chunk = pltpu.VMEM((2, 2, HALF, D), BF16)
    hid = pltpu.VMEM((2, 2, FF, HALF), BF16)
    g_in, g_out, p_out = pl.pallas_call(
        kernel,
        out_shape=(grad, grad, jax.ShapeDtypeStruct((2, TOK, 2), BF16)),
        in_specs=[anyspace] * 4 + [vmem] * 2,
        out_specs=(anyspace, anyspace, vmem),
        scratch_shapes=[
            pltpu.VMEM((2, TOK, D), BF16), pltpu.VMEM((TOK, D), BF16), weight, weight,
            wide, wide, wide, wide,
            wide, wide, wide, wide, wide,
            chunk, chunk, hid, hid,
            pltpu.VMEM((2, FF, HALF), F32), pltpu.VMEM((HALF, FF), BF16),
            pltpu.VMEM((64, D), BF16),
            pltpu.VMEM((FF, D), F32), pltpu.VMEM((FF, D), F32), weight, weight,
            pltpu.VMEM((TOK, D), BF16), pltpu.VMEM((TOK, D), BF16),
            pltpu.VMEM((ROWS, 128), BF16), pltpu.VMEM((ROWS, 128), BF16),
            pltpu.VMEM((3, ROWS, TOK), BF16), pltpu.VMEM((3, ROWS, TOK), BF16),
            pltpu.VMEM((3, TOK, ROWS), BF16), pltpu.VMEM((2, TOK, 128), F32),
            pltpu.SemaphoreType.DMA((6, PEERS)), pltpu.SemaphoreType.DMA((6, PEERS)),
            pltpu.SemaphoreType.DMA, pltpu.SemaphoreType.DMA,
            pltpu.SemaphoreType.DMA((4,)), pltpu.SemaphoreType.DMA((2, 8)),
        ],
        compiler_params=pltpu.CompilerParams(
            collective_id=0, has_side_effects=True, vmem_limit_bytes=64 * 1024 * 1024 - 65536
        ),
        name="relay",
    )(inputs[0], entering[0], weight_in[0, 0], weight_out[0, 0], gate_probs[0], expert_ids[0])
    return (g_in[None, None], g_out[None, None], p_out[None])


def solution(mesh):
    return jax.shard_map(
        body,
        mesh=mesh,
        in_specs=(
            P("segment", None, "expert", None),
            P("segment", "expert", None),
            P("segment", "expert", None, None),
            P("segment", "expert", None, None),
            P("segment", None, "expert", None),
            P("segment", None, "expert", None),
        ),
        out_specs=(
            P("segment", "expert", None, None),
            P("segment", "expert", None, None),
            P("segment", None, "expert", None),
        ),
        check_vma=False,
    )
```

```python
import jax
import jax.numpy as jnp
from jax import lax
from jax.experimental import pallas as pl
from jax.experimental.pallas import tpu as pltpu
from jax.sharding import PartitionSpec as P

MESH = pl.DeviceIdType.MESH
F32 = jnp.float32
BF16 = jnp.bfloat16
NT = (((1,), (1,)), ((), ()))
FF = 704
D = 2048
TOK = 128
PEERS = 32
ROWS = 256
WIDE = 3072
HALF = 192
HR = 0.7071067811865476
DS = 0.3989422804014327


def iota(shape, dim):
    return lax.broadcasted_iota(jnp.int32, shape, dim)


def dot(a, b):
    return jnp.dot(a, b, preferred_element_type=F32)


def dot_nt(a, b):
    return lax.dot_general(a, b, NT, preferred_element_type=F32)


def onehot(cond):
    return jnp.where(cond, 1.0, 0.0)


def kernel(
    inputs_hbm, entering_hbm, win_hbm, wout_hbm, probs_ref, ids_ref,
    gin_ref, gout_ref, pg_ref,
    xin, g0, win, wout,
    sx0, sg, sx1, rs,
    xr0, gr0, xr1, rr, gr1,
    xc, gc, ht, gp, slope, gpr, rb,
    acco, acci,
    lv_send, lv_recv, s_send, s_recv,
    da, dap, ca, cols,
    send_sem, recv_sem, z_send, z_recv, local_sem,
):
    me = lax.axis_index("expert")
    seg = lax.axis_index("segment")
    core = lax.rem(me, 2)
    px = lax.rem(lax.div(me, 2), 4)
    py = lax.div(me, 8)

    def steps(k):
        dc = lax.rem(k, 2)
        dx = lax.rem(lax.div(k, 2), 4)
        dy = lax.rem(lax.div(k, 8) + dx, 4)
        return dy, dx, dc

    def ahead(k):
        dy, dx, dc = steps(k)
        return lax.rem(py + dy, 4) * 8 + lax.rem(px + dx, 4) * 2 + lax.rem(core + dc, 2)

    def behind(k):
        dy, dx, dc = steps(k)
        return lax.rem(py + 4 - dy, 4) * 8 + lax.rem(px + 4 - dx, 4) * 2 + lax.rem(core + dc, 2)

    def copy(stage, src, dst, k, peer):
        rows = pl.ds(pl.multiple_of(k * 8, 8), 8)
        return pltpu.make_async_remote_copy(
            src_ref=src.at[rows], dst_ref=dst.at[rows],
            send_sem=send_sem.at[stage, k], recv_sem=recv_sem.at[stage, k],
            device_id=(seg, peer), device_id_type=MESH,
        )

    def send(stage, src, dst, route, low, high):
        def one(k, carry):
            copy(stage, src, dst, k, route(k)).start()
            return carry
        lax.fori_loop(max(low, 1), high, one, 0)

    def arrive(stage, src, dst, low, high):
        def one(k, carry):
            copy(stage, src, dst, k, ahead(k)).wait_recv()
            return carry
        lax.fori_loop(max(low, 1), high, one, 0)

    def sent(stage, src, dst):
        def one(k, carry):
            copy(stage, src, dst, k, ahead(k)).wait_send()
            return carry
        lax.fori_loop(1, PEERS, one, 0)

    load_g = pltpu.make_async_copy(entering_hbm, g0, local_sem.at[0])
    load_x = pltpu.make_async_copy(inputs_hbm, xin, local_sem.at[1])
    load_wi = pltpu.make_async_copy(win_hbm, win, local_sem.at[2])
    load_wo = pltpu.make_async_copy(wout_hbm, wout, local_sem.at[3])
    load_x.start()
    load_g.start()
    load_wi.start()
    load_wo.start()

    barrier = pltpu.get_barrier_semaphore()

    def greet(k, carry):
        pl.semaphore_signal(barrier, inc=1, device_id=(seg, ahead(k)), device_id_type=MESH)
        return carry

    lax.fori_loop(1, PEERS, greet, 0)
    below = lax.rem(seg + 7, 8)
    above = lax.rem(seg + 1, 8)
    pl.semaphore_signal(barrier, inc=1, device_id=(below, me), device_id_type=MESH)
    pl.semaphore_signal(barrier, inc=1, device_id=(above, me), device_id_type=MESH)

    def places(tick):
        row = iota((8, 128), 0)
        ids = ids_ref[tick].astype(F32)
        odds = probs_ref[tick].astype(F32)
        table = jnp.where(row == 0, ids[0:1], jnp.where(row == 1, ids[1:2], 0.0))
        table = jnp.where(row == 2, odds[0:1], jnp.where(row == 3, odds[1:2], table))
        turn = onehot(iota((TOK, 128), 0) == iota((TOK, 128), 1)).astype(BF16)
        columns = dot_nt(turn, table.astype(BF16))
        k = iota((TOK, 128), 1)
        dx = (k >> 1) & 3
        dy = ((k >> 3) + dx) & 3
        owner = ((py + dy) & 3) * 8 + ((px + dx) & 3) * 2 + ((core + (k & 1)) & 1)
        owner = jnp.where(k < PEERS, owner, -1).astype(F32)
        named = [columns[:, j : j + 1] == owner for j in range(2)]
        either = onehot(named[0] | named[1]).astype(BF16)
        earlier = onehot(iota((TOK, TOK), 1) < iota((TOK, TOK), 0)).astype(BF16)
        count = dot(earlier, either)
        first = (k * 8).astype(F32)
        packed = jnp.zeros((TOK, 128), F32)
        for j in range(2):
            rank = jnp.sum(jnp.where(named[j], count, 0.0), axis=1, keepdims=True)
            base = jnp.sum(jnp.where(named[j], first, 0.0), axis=1, keepdims=True)
            low = jnp.where(rank < 8.0, base + rank, -100.0)
            high = jnp.where(rank < 8.0, -100.0, base + rank - 8.0)
            packed = jnp.where(k == j, low, packed)
            packed = jnp.where(k == 2 + j, high, packed)
            packed = jnp.where(k == 4 + j, columns[:, 2 + j : 3 + j], packed)
        cols[tick] = packed
        eye = onehot(iota((8, 128), 0) == iota((8, 128), 1)).astype(BF16)
        turned = dot_nt(eye, packed.astype(BF16))
        slot = iota((ROWS, TOK), 0).astype(F32)
        for part, (row, shift) in enumerate(((0, 0.0), (2, 0.0), (2, 4.0))):
            hit0 = slot == turned[row : row + 1] + shift
            hit1 = slot == turned[row + 1 : row + 2] + shift
            da[part] = onehot(hit0 | hit1).astype(BF16)
            dap[part] = jnp.where(
                hit0, turned[4:5], jnp.where(hit1, turned[5:6], 0.0)
            ).astype(BF16)

    def pick(tick, j, part):
        row, shift = ((0, 0.0), (2, 0.0), (2, 4.0))[part]
        slot = iota((TOK, ROWS), 1).astype(F32)
        return slot == cols[tick, :, row + j : row + j + 1] + shift

    def dispatch(mats, rows, dst):
        for n in range(4):
            c = slice(n * 512, n * 512 + 512)
            dst[:, c] = dot(mats[0], rows[:, c]).astype(BF16)
        for n in range(2):
            c = slice(n * 512, n * 512 + 512)
            h = slice(1024 + n * 512, 1536 + n * 512)
            dst[:, 2048 + n * 512 : 2560 + n * 512] = (
                dot(mats[1], rows[:, c]) + dot(mats[2], rows[:, h])
            ).astype(BF16)

    def split_matrix():
        o = iota((128, 128), 0)
        i = iota((128, 128), 1)
        return onehot(i == ((o & 63) >> 2) * 8 + (o >> 6) * 4 + (o & 3)).astype(BF16)

    def join_matrix():
        i = iota((128, 128), 0)
        o = iota((128, 128), 1)
        return onehot(i == ((o & 63) >> 2) * 8 + (o >> 6) * 4 + (o & 3)).astype(BF16)

    def gather(src, dst, tick, h):
        r = slice(h * 128, h * 128 + 128)
        dst[tick, h, 0:128, :] = src[r, 0:D]
        for n in range(2):
            b = dot(split_matrix(), src[r, D + n * 512 : D + n * 512 + 512]).astype(BF16)
            dst[tick, h, 128:192, n * 512 : n * 512 + 512] = b[0:64]
            dst[tick, h, 128:192, 1024 + n * 512 : 1536 + n * 512] = b[64:128]

    def forward(tick, h):
        def tile(m, carry):
            r = pl.ds(pl.multiple_of(m * 352, 16), 352)
            pre = dot_nt(win[r, :], xc[tick, h])
            cdf = 0.5 * (1.0 + lax.erf(pre * HR))
            pdf = DS * jnp.exp(-0.5 * pre * pre)
            ht[tick, h, r, :] = (pre * cdf).astype(BF16)
            slope[h, r, :] = cdf + pre * pdf
            return carry
        lax.fori_loop(0, 2, tile, 0)

    def backward(tick, h):
        def tile(m, total):
            r = pl.ds(pl.multiple_of(m * 352, 16), 352)
            q = dot_nt(wout[r, :], gc[tick, h])
            gp[tick, h, r, :] = (q * slope[h, r, :]).astype(BF16)
            return total + jnp.sum(ht[tick, h, r, :].astype(F32) * q, axis=0, keepdims=True)
        s = lax.fori_loop(0, 2, tile, jnp.zeros((1, HALF), F32))
        i = iota((128, HALF), 0)
        r = iota((128, HALF), 1)
        ones = jnp.ones((HALF, 128), BF16)
        sa = dot(jnp.where(r == i, s, 0.0).astype(BF16), ones)
        tail = ((i & 7) < 4) & (r == 128 + (i >> 3) * 4 + (i & 7))
        sb = dot(jnp.where(tail, s, 0.0).astype(BF16), ones)
        lane = iota((128, 128), 1)
        rows = slice(h * 128, h * 128 + 128)
        before = jnp.zeros((128, 128), F32) if tick == 0 else s_send[rows, :].astype(F32)
        s_send[rows, :] = jnp.where(
            lane == tick, sa, jnp.where(lane == 2 + tick, sb, before)
        ).astype(BF16)

    def give_back(h):
        eye = onehot(iota((HALF, HALF), 0) == iota((HALF, HALF), 1)).astype(BF16)
        gpr[...] = dot_nt(eye, gp[0, h]).astype(BF16)
        rows = slice(h * 128, h * 128 + 128)

        def tile(n, carry):
            c = pl.ds(pl.multiple_of(n * 512, 512), 512)
            r = dot(gpr[...], win[:, c]).astype(BF16)
            rs[rows, c] = r[0:128]
            rb[:, c] = r[128:192]
            return carry

        lax.fori_loop(0, 4, tile, 0)
        join = join_matrix()
        for n in range(2):
            c = slice(n * 512, n * 512 + 512)
            d = slice(1024 + n * 512, 1536 + n * 512)
            b = dot(join[:, 0:64], rb[:, c]) + dot(join[:, 64:128], rb[:, d])
            rs[rows, D + n * 512 : D + n * 512 + 512] = b.astype(BF16)

    def own(src, dst):
        dst[0:8, :] = src[0:8, :]

    places(0)
    load_x.wait()
    dispatch([da[0], da[1], da[2]], xin.at[0], sx0)
    pl.semaphore_wait(barrier, PEERS + 1)
    send(0, sx0, xr0, ahead, 0, PEERS)
    load_g.wait()
    dispatch([dap[0], dap[1], dap[2]], g0, sg)
    send(1, sg, gr0, ahead, 0, PEERS)
    own(sx0, xr0)
    own(sg, gr0)
    for part in range(3):
        ca[part] = onehot(pick(0, 0, part) | pick(0, 1, part)).astype(BF16)
    places(1)
    dispatch([da[0], da[1], da[2]], xin.at[1], sx1)
    own(sx1, xr1)
    load_wi.wait()
    load_wo.wait()

    for h in range(2):
        arrive(0, sx0, xr0, h * 16, h * 16 + 16)
        gather(xr0, xc, 0, h)
        forward(0, h)
    for h in range(2):
        arrive(1, sg, gr0, h * 16, h * 16 + 16)
        gather(gr0, gc, 0, h)
        backward(0, h)
        give_back(h)
        send(2, rs, rr, behind, h * 16, h * 16 + 16)
    own(rs, rr)
    send(3, sx1, xr1, ahead, 0, PEERS)

    def first_sums(n, carry):
        c = pl.ds(pl.multiple_of(n * 256, 256), 256)
        acco[:, c] = dot(ht[0, 0], gc[0, 0, :, c]) + dot(ht[0, 1], gc[0, 1, :, c])
        acci[:, c] = dot(gp[0, 0], xc[0, 0, :, c]) + dot(gp[0, 1], xc[0, 1, :, c])
        return carry

    lax.fori_loop(0, 8, first_sums, 0)

    arrive(2, rs, rr, 0, PEERS)
    for n in range(4):
        c = slice(n * 512, n * 512 + 512)
        d = slice(D + (n % 2) * 512, D + (n % 2) * 512 + 512)
        total = g0[:, c].astype(F32) + dot(ca[0], rr[:, c]) + dot(ca[1 + n // 2], rr[:, d])
        lv_send[:, c] = total.astype(BF16)
    relay = pltpu.make_async_remote_copy(
        src_ref=lv_send, dst_ref=lv_recv, send_sem=z_send, recv_sem=z_recv,
        device_id=(below, me), device_id_type=MESH,
    )
    relay.start()
    sent(1, sg, gr0)
    relay.wait_recv()
    for n in range(4):
        c = slice(n * 512, n * 512 + 512)
        v = lv_recv[:, c]
        g0[:, c] = jnp.where(seg == 7, jnp.zeros_like(v), v)
    dispatch([dap[0], dap[1], dap[2]], g0, sg)
    send(4, sg, gr1, ahead, 0, PEERS)
    own(sg, gr1)

    for h in range(2):
        arrive(3, sx1, xr1, h * 16, h * 16 + 16)
        gather(xr1, xc, 1, h)
        forward(1, h)

    arrive(4, sg, gr1, 0, 16)
    gather(gr1, gc, 1, 0)
    backward(1, 0)

    def more_sums(n, carry):
        c = pl.ds(pl.multiple_of(n * 256, 256), 256)
        acco[:, c] += dot(ht[1, 0], gc[1, 0, :, c])
        acci[:, c] += dot(gp[1, 0], xc[1, 0, :, c])
        return carry

    lax.fori_loop(0, 8, more_sums, 0)

    arrive(4, sg, gr1, 16, PEERS)
    gather(gr1, gc, 1, 1)
    backward(1, 1)
    send(5, s_send, s_recv, behind, 0, PEERS)
    own(s_send, s_recv)

    def last_sums(n, carry):
        c = pl.ds(pl.multiple_of(n * 256, 256), 256)
        gout_ref[:, c] = (acco[:, c] + dot(ht[1, 1], gc[1, 1, :, c])).astype(BF16)
        gin_ref[:, c] = (acci[:, c] + dot(gp[1, 1], xc[1, 1, :, c])).astype(BF16)
        return carry

    lax.fori_loop(0, 8, last_sums, 0)

    arrive(5, s_send, s_recv, 0, PEERS)
    lane = iota((TOK, 128), 1)
    score = s_recv[...]
    found = jnp.zeros((TOK, 128), F32)
    for tick in range(2):
        for j in range(2):
            va = dot(onehot(pick(tick, j, 0)).astype(BF16), score)
            vb = dot(onehot(pick(tick, j, 1)).astype(BF16), score)
            both = jnp.where(lane == tick, va, 0.0) + jnp.where(lane == 2 + tick, vb, 0.0)
            value = jnp.sum(both, axis=1, keepdims=True) / cols[tick, :, 4 + j : 5 + j]
            found = jnp.where(lane == 2 * tick + j, value, found)
    eye = onehot(iota((8, 128), 0) == iota((8, 128), 1)).astype(BF16)
    turned = dot_nt(eye, found.astype(BF16)).astype(BF16)
    for tick in range(2):
        pg_ref[tick] = turned[2 * tick : 2 * tick + 2]

    relay.wait_send()
    sent(0, sx0, xr0)
    sent(2, rs, rr)
    sent(3, sx1, xr1)
    sent(4, sg, gr1)
    sent(5, s_send, s_recv)


def body(inputs, entering, weight_in, weight_out, gate_probs, expert_ids):
    anyspace = pl.BlockSpec(memory_space=pl.ANY)
    vmem = pl.BlockSpec(memory_space=pltpu.VMEM)
    wide = pltpu.VMEM((ROWS, WIDE), BF16)
    weight = pltpu.VMEM((FF, D), BF16)
    grad = pltpu.VMEM((FF, D), BF16)
    chunk = pltpu.VMEM((2, 2, HALF, D), BF16)
    hid = pltpu.VMEM((2, 2, FF, HALF), BF16)
    g_in, g_out, p_out = pl.pallas_call(
        kernel,
        out_shape=(grad, grad, pltpu.VMEM((2, 2, TOK), BF16)),
        in_specs=[anyspace] * 4 + [vmem] * 2,
        out_specs=(vmem, vmem, vmem),
        scratch_shapes=[
            pltpu.VMEM((2, TOK, D), BF16), pltpu.VMEM((TOK, D), BF16), weight, weight,
            wide, wide, wide, wide,
            wide, wide, wide, wide, wide,
            chunk, chunk, hid, hid,
            pltpu.VMEM((2, FF, HALF), F32), pltpu.VMEM((HALF, FF), BF16),
            pltpu.VMEM((64, D), BF16),
            pltpu.VMEM((FF, D), F32), pltpu.VMEM((FF, D), F32),
            pltpu.VMEM((TOK, D), BF16), pltpu.VMEM((TOK, D), BF16),
            pltpu.VMEM((ROWS, 128), BF16), pltpu.VMEM((ROWS, 128), BF16),
            pltpu.VMEM((3, ROWS, TOK), BF16), pltpu.VMEM((3, ROWS, TOK), BF16),
            pltpu.VMEM((3, TOK, ROWS), BF16), pltpu.VMEM((2, TOK, 128), F32),
            pltpu.SemaphoreType.DMA((6, PEERS)), pltpu.SemaphoreType.DMA((6, PEERS)),
            pltpu.SemaphoreType.DMA, pltpu.SemaphoreType.DMA,
            pltpu.SemaphoreType.DMA((4,)),
        ],
        compiler_params=pltpu.CompilerParams(
            collective_id=0, has_side_effects=True, vmem_limit_bytes=48 * 1024 * 1024
        ),
        name="relay",
    )(inputs[0], entering[0], weight_in[0, 0], weight_out[0, 0],
      jnp.swapaxes(gate_probs[0], 1, 2), jnp.swapaxes(expert_ids[0], 1, 2))
    return (g_in[None, None], g_out[None, None], jnp.swapaxes(p_out, 1, 2)[None])


def solution(mesh):
    return jax.shard_map(
        body,
        mesh=mesh,
        in_specs=(
            P("segment", None, "expert", None),
            P("segment", "expert", None),
            P("segment", "expert", None, None),
            P("segment", "expert", None, None),
            P("segment", None, "expert", None),
            P("segment", None, "expert", None),
        ),
        out_specs=(
            P("segment", "expert", None, None),
            P("segment", "expert", None, None),
            P("segment", None, "expert", None),
        ),
        check_vma=False,
    )
```
